32 devices in a mesh: rows: 8 (over y, x, core), heads: 4 (over z).
Axes of the slice: x: 2, y: 2, z: 4, core: 2. Of those that a mesh axis runs over, the one named last changes fastest.
Arguments:
- test_rows: bfloat16 [1024, 512], P('rows'), may hold values from -6 to 6
- query_weight: bfloat16 [512, 512], P(None, 'heads'), may hold values from -0.54120401 to 0.54120401
- keys: bfloat16 [32768, 512], P('rows', 'heads'), may hold values from -8 to 8
- values: bfloat16 [32768, 512], P('rows', 'heads'), may hold values from -6 to 6
- out_weight: bfloat16 [512, 512], P('heads'), may hold values from -0.25 to 0.25
Outputs:
- mixed: bfloat16 [1024, 512], P('rows', 'heads')
The draws below stay inside these ranges and needn't reach their ends.
All inputs are finite; a program needn't handle non-finite values.
Results may differ from the reference program's by a relative error of at most 0.0079.
Values may be sent and summed in bfloat16 or wider, within the bound.
A program may use at most 64 MiB of HBM per device.

```python
import jax
import jax.numpy as jnp
from jax import lax

D = 512
HEADS = 8
HEAD_DIM = 64
TEST_DEV = 128
CTX_DEV = 4096
NTEST = 1024
NCTX = 32768


def weight_common(seed_key):
    spread = (D // 9) ** (-0.5)
    raw = jnp.clip(jax.random.normal(jax.random.fold_in(seed_key, 301), (D, D), jnp.float32), -4.0, 4.0)
    return raw * spread


def planted_layout(seed_key):
    shard_count = NTEST // TEST_DEV
    position = jnp.arange(shard_count)
    chosen = position % 4 == jax.random.randint(jax.random.fold_in(seed_key, 311), (), 0, 4)
    within = jax.random.randint(jax.random.fold_in(seed_key, 312), (), 0, TEST_DEV)
    test_index = position * TEST_DEV + within
    offset = jax.random.randint(jax.random.fold_in(seed_key, 313), (), 1, shard_count)
    first_slot = jax.random.randint(jax.random.fold_in(seed_key, 314), (), 0, CTX_DEV // 2)
    second_slot = jax.random.randint(jax.random.fold_in(seed_key, 315), (), CTX_DEV // 2, CTX_DEV)
    first_index = (position + offset) % shard_count * CTX_DEV + first_slot
    second_index = (position + offset) % shard_count * CTX_DEV + second_slot
    strength = 0.8 + 0.2 * position.astype(jnp.float32) / (shard_count - 1)
    spacing = jax.random.uniform(jax.random.fold_in(seed_key, 316), (shard_count,), jnp.float32, 1.2, 2.8)
    coins = jax.random.bernoulli(jax.random.fold_in(seed_key, 317), 0.5, (shard_count, D))
    pattern = jnp.where(coins, 6.0, -6.0).astype(jnp.float32)
    return (chosen, test_index, first_index, second_index, strength, spacing, pattern)


def draw_query_weight(key, part):
    return weight_common(key).astype(jnp.bfloat16)


def draw_test_rows(key, part):
    raw = jnp.clip(jax.random.normal(jax.random.fold_in(key, 321), (NTEST, D), jnp.float32), -6.0, 6.0)
    layout = planted_layout(key)
    chosen = layout[0]
    test_index = layout[1]
    pattern = layout[6]
    hits = ((jnp.arange(NTEST)[:, None] == test_index[None, :]) & chosen[None, :]).astype(jnp.float32)
    planted = jnp.dot(hits, pattern, precision=lax.Precision.HIGHEST)
    marked = jnp.sum(hits, axis=1, keepdims=True) > 0.5
    return jnp.where(marked, planted, raw).astype(jnp.bfloat16)


def draw_keys(key, part):
    raw = jnp.clip(jax.random.normal(jax.random.fold_in(key, 331), (NCTX, D), jnp.float32), -6.0, 6.0)
    chosen, test_index, first_index, second_index, strength, spacing, pattern = planted_layout(key)
    shard_count = pattern.shape[0]
    weight = weight_common(key)
    queries = jnp.dot(pattern, weight, precision=lax.Precision.HIGHEST).reshape(shard_count, HEADS, HEAD_DIM)
    peak = jnp.max(jnp.abs(queries), axis=2, keepdims=True)
    first_rows = 8.0 * strength[:, None, None] * queries / peak
    at_peak = (jnp.abs(queries) >= peak).astype(jnp.float32)
    divisor = jnp.where(at_peak > 0.5, queries, 1.0)
    second_rows = first_rows - at_peak * spacing[:, None, None] * HEAD_DIM ** 0.5 / divisor
    first_rows = first_rows.reshape(shard_count, D)
    second_rows = second_rows.reshape(shard_count, D)
    row_ids = jnp.arange(NCTX)[:, None]
    first_hits = ((row_ids == first_index[None, :]) & chosen[None, :]).astype(jnp.float32)
    second_hits = ((row_ids == second_index[None, :]) & chosen[None, :]).astype(jnp.float32)
    planted = jnp.dot(first_hits, first_rows, precision=lax.Precision.HIGHEST)
    planted = planted + jnp.dot(second_hits, second_rows, precision=lax.Precision.HIGHEST)
    marked = jnp.sum(first_hits + second_hits, axis=1, keepdims=True) > 0.5
    return jnp.where(marked, planted, raw).astype(jnp.bfloat16)


def steps_of(own_key, dims, pieces, low, high):
    def one(dim, shards_of):
        draws = jax.random.uniform(jax.random.fold_in(jax.random.fold_in(own_key, 6), dim), (shards_of,), jnp.float32, low / len(pieces), high / len(pieces))
        return jnp.repeat(jnp.exp(draws), dims[dim] // shards_of).reshape((-1,) + (1,) * (len(dims) - dim - 1))

    gain = one(*pieces[0])
    for cut in pieces[1:]:
        gain = gain * one(*cut)
    return gain


def bell_draw(key, extent, deviation, most, split=(), dtype=jnp.bfloat16):
    values = deviation * jax.random.normal(key, extent, jnp.float32)
    if split:
        values = values * steps_of(key, extent, split, -0.22, 0.18)
    return jnp.clip(values, -most, most).astype(dtype)


def setup_inputs(seed: int = 0) -> dict:
    arg_keys = jax.random.split(jax.random.key(seed), 6)
    test_rows = draw_test_rows(jax.random.fold_in(arg_keys[5], 71), 0)
    query_weight = draw_query_weight(jax.random.fold_in(arg_keys[5], 71), 0)
    keys = draw_keys(jax.random.fold_in(arg_keys[5], 71), 0)
    values = bell_draw(arg_keys[3], (NCTX, D), 1.0, 6.0, ((0, 8), (1, 4)))
    out_weight = bell_draw(arg_keys[4], (D, D), D ** -0.5, 0.25, ((0, 4),))
    return {"test_rows": test_rows, "query_weight": query_weight, "keys": keys, "values": values, "out_weight": out_weight}


def reference(test_rows, query_weight, keys, values, out_weight):
    query = jnp.dot(test_rows, query_weight, preferred_element_type=jnp.float32).astype(jnp.bfloat16)
    count = query.shape[0]
    block = min(512, count)
    factor = HEAD_DIM ** -0.5

    def one_head(head):
        start = (head * HEAD_DIM).astype(jnp.int32)
        query_head = lax.dynamic_slice_in_dim(query, start, HEAD_DIM, 1)
        key_head = lax.dynamic_slice_in_dim(keys, start, HEAD_DIM, 1)
        value_head = lax.dynamic_slice_in_dim(values, start, HEAD_DIM, 1)

        def one_block(number):
            first = (number * block).astype(jnp.int32)
            query_block = lax.dynamic_slice_in_dim(query_head, first, block, 0)
            scores = jnp.dot(query_block, key_head.T, preferred_element_type=jnp.float32) * factor
            largest = jnp.max(scores, axis=1, keepdims=True)
            weights = jnp.exp(scores - largest)
            total = jnp.sum(weights, axis=1, keepdims=True)
            summed = jnp.dot(weights.astype(jnp.bfloat16), value_head, preferred_element_type=jnp.float32)
            return (summed / total).astype(jnp.bfloat16)

        blocks = lax.map(one_block, jnp.arange(count // block).astype(jnp.int32))
        return blocks.reshape(count, HEAD_DIM)

    per_head = lax.map(one_head, jnp.arange(HEADS).astype(jnp.int32))
    attended = per_head.transpose(1, 0, 2).reshape(count, HEADS * HEAD_DIM)
    return jnp.dot(attended, out_weight, preferred_element_type=jnp.float32).astype(jnp.bfloat16)
```

```python
import functools
import math

import jax
import jax.numpy as jnp
from jax import lax
from jax.experimental import pallas as pl
from jax.experimental.pallas import tpu as pltpu
from jax.sharding import PartitionSpec as P

HEAD_DIM = 64
LOG2E = math.log2(math.e)
MESH = pl.DeviceIdType.MESH
CHUNK = 512


def xor_of(a, b, count):
    total = 0
    bit = 1
    while bit < count:
        one = (a // bit) % 2
        two = (b // bit) % 2
        total = total + bit * (one + two - 2 * one * two)
        bit *= 2
    return total


def near_masks(n):
    return [m for m in range(1, n) if (m >> 1) & ((m >> 1) - 1) == 0]


def turn_order(n):
    near = near_masks(n)
    far = [m for m in range(1, n) if m not in near]
    return near[:3] + far + near[:2:-1]


def peer_of(me, step, n):
    if isinstance(step, int):
        return xor_of(me, turn_order(n)[step - 1], n)
    mask = 0
    for i, m in enumerate(turn_order(n)):
        mask = jnp.where(step == i + 1, m, mask)
    return xor_of(me, mask, n)


def kernel(
    n, nz, chunk,
    x_hbm, wq_hbm, k_hbm, v_hbm, wo_hbm, o_ref,
    x_ref, wq_ref, k_ref, v_ref, wo_ref, vt_ref, qall, s0, s1,
    num_out, stat_out, num_in, stat_in, att, wo_in,
    in_sem, row_sem, col_sem, q_send, q_recv, n_send, n_recv, t_send, t_recv, a_send, a_recv, w_send, w_recv,
):
    me = lax.axis_index("rows")
    mz = lax.axis_index("heads")
    count = x_ref.shape[0]
    ctx, width = k_ref.shape
    cols = o_ref.shape[1]
    f32, bf = jnp.float32, jnp.bfloat16
    chunks = [pl.ds(c, chunk) for c in range(0, ctx, chunk)]

    loads = [
        pltpu.make_async_copy(src, dst, in_sem.at[i])
        for i, (src, dst) in enumerate([
            (x_hbm, x_ref), (wq_hbm, wq_ref), (k_hbm, k_ref), (v_hbm, v_ref), (wo_hbm, wo_ref)])]
    for load in loads:
        load.start()

    near = near_masks(n)
    below = (mz + nz - 1) // nz
    above = (2 * nz - 2 - mz) // nz

    def tell_columns(sem):
        @pl.when(mz > 0)
        def _():
            pl.semaphore_signal(sem, inc=1, device_id={"heads": mz - 1}, device_id_type=MESH)

        @pl.when(mz < nz - 1)
        def _():
            pl.semaphore_signal(sem, inc=1, device_id={"heads": mz + 1}, device_id_type=MESH)

    def tell_rows(sem):
        for m in spread_by:
            pl.semaphore_signal(sem, inc=1, device_id={"rows": xor_of(me, m, n)}, device_id_type=MESH)

    spread_by = [m for m in near if m > 1 and m % 2 == 0]
    barrier = pltpu.get_barrier_semaphore()
    for m in near:
        pl.semaphore_signal(barrier, inc=1, device_id={"rows": xor_of(me, m, n)}, device_id_type=MESH)
    tell_columns(barrier)

    loads[0].wait()
    loads[1].wait()
    q = jnp.dot(x_ref[...], wq_ref[...], preferred_element_type=f32).astype(bf)
    qall[me] = q * jnp.bfloat16(HEAD_DIM ** -0.5)

    def q_copy(peer, slot):
        return pltpu.make_async_remote_copy(
            src_ref=qall.at[me], dst_ref=qall.at[slot], send_sem=q_send.at[peer],
            recv_sem=q_recv.at[slot], device_id={"rows": peer}, device_id_type=MESH)

    def w_copy(i):
        peer = (mz + i) % nz
        return pltpu.make_async_remote_copy(
            src_ref=wo_ref.at[:, pl.ds(pl.multiple_of(peer * cols, cols), cols)],
            dst_ref=wo_in.at[mz], send_sem=w_send.at[i], recv_sem=w_recv.at[mz],
            device_id={"heads": peer}, device_id_type=MESH)

    lane = lax.broadcasted_iota(jnp.int32, (1, width), 1)
    keep0 = jnp.where(lane < HEAD_DIM, 1.0, 0.0).astype(bf)
    keep1 = jnp.where(lane < HEAD_DIM, 0.0, 1.0).astype(bf)

    def both_heads(peer):
        q = qall[peer]
        return jnp.concatenate([q * keep0, q * keep1], axis=0)

    def score(both, part, s_ref, top):
        s = lax.dot_general(k_ref[part, :], both, (((1,), (1,)), ((), ())), preferred_element_type=f32)
        s_ref[part, :] = s
        here = jnp.max(s, axis=0, keepdims=True)
        return here if top is None else jnp.maximum(top, here)

    def weigh(s_ref, part, top, total, acc):
        w = jnp.exp2((s_ref[part, :] - top) * LOG2E)
        here = jnp.sum(w, axis=0, keepdims=True)
        summed = jnp.dot(vt_ref[:, part], w.astype(bf), preferred_element_type=f32)
        return (here, summed) if total is None else (total + here, acc + summed)

    def keep(peer, top, total, acc):
        num = jnp.concatenate([acc[:HEAD_DIM, :count], acc[HEAD_DIM:, count:]], axis=0)
        num_out[peer] = num.astype(num_out.dtype)
        stat_out[peer, 0:1, :] = top[:, :count]
        stat_out[peer, 1:2, :] = top[:, count:]
        stat_out[peer, 2:3, :] = total[:, :count]
        stat_out[peer, 3:4, :] = total[:, count:]

    def turn(now, s_now, top, later, s_later):
        both = None if later is None else both_heads(later)
        after = total = acc = None
        for part in chunks:
            if both is not None:
                after = score(both, part, s_later, after)
            total, acc = weigh(s_now, part, top, total, acc)
        keep(now, top, total, acc)
        return after

    def n_copy(peer, slot):
        return pltpu.make_async_remote_copy(
            src_ref=num_out.at[peer], dst_ref=num_in.at[slot], send_sem=n_send.at[peer],
            recv_sem=n_recv.at[slot], device_id={"rows": peer}, device_id_type=MESH)

    def t_copy(peer, slot):
        return pltpu.make_async_remote_copy(
            src_ref=stat_out.at[peer], dst_ref=stat_in.at[slot], send_sem=t_send.at[peer],
            recv_sem=t_recv.at[slot], device_id={"rows": peer}, device_id_type=MESH)

    def send(peer):
        n_copy(peer, me).start()
        t_copy(peer, me).start()

    def await_q(step):
        peer = peer_of(me, step, n)
        q_copy(peer, peer).wait_recv()
        return peer

    stat_out[...] = jnp.zeros(stat_out.shape, f32)
    pl.semaphore_wait(barrier, len(near) + below + above)
    if len(spread_by) > 1:
        tell_rows(row_sem.at[0])
    if nz > 2:
        tell_columns(col_sem.at[0])
    for m in turn_order(n):
        if m in near:
            q_copy(xor_of(me, m, n), me).start()

    loads[2].wait()
    loads[3].wait()
    both = both_heads(me)
    top = None
    for part in chunks:
        top = score(both, part, s0, top)
        vt_ref[:, part] = v_ref[part, :].T

    for i in range(len(spread_by) - 1):
        pl.semaphore_wait(row_sem.at[i], len(spread_by))
        if i + 1 < len(spread_by) - 1:
            tell_rows(row_sem.at[i + 1])
    for m in turn_order(n):
        if m not in near:
            q_copy(xor_of(me, m, n), me).start()
    for i in range(nz - 3):
        pl.semaphore_wait(col_sem.at[i], below + above)
        tell_columns(col_sem.at[i + 1])

    turn(me, s0, top, None, None)

    both = both_heads(await_q(1))
    top = None
    for part in chunks:
        top = score(both, part, s1, top)

    def share_weights():
        if nz > 2:
            pl.semaphore_wait(col_sem.at[nz - 3], below + above)
        loads[4].wait()
        for i in range(1, nz):
            w_copy(i).start()

    def two(pair, top):
        step = 2 * pair + 1
        now, later = peer_of(me, step, n), await_q(step + 1)
        top = turn(now, s1, top, later, s0)
        send(now)

        @pl.when(pair == 0)
        def _():
            share_weights()

        now, later = later, await_q(step + 2)
        top = turn(now, s0, top, later, s1)
        send(now)
        return top

    if n == 2:
        share_weights()
    top = lax.fori_loop(0, (n - 2) // 2, two, top)
    last = peer_of(me, n - 1, n)
    turn(last, s1, top, None, None)
    send(last)

    def parts(peer, num_ref, stat_ref):
        return (num_ref[peer].astype(f32), stat_ref[peer, 0:2, :], stat_ref[peer, 2:4, :])

    def spread(pair):
        return jnp.concatenate([
            jnp.broadcast_to(pair[0:1, :], (HEAD_DIM, count)),
            jnp.broadcast_to(pair[1:2, :], (HEAD_DIM, count))], axis=0)

    def merge(step, state):
        num, m, l = state
        peer = peer_of(me, step, n)
        n_copy(peer, peer).wait_recv()
        t_copy(peer, peer).wait_recv()
        num2, m2, l2 = parts(peer, num_in, stat_in)
        top = jnp.maximum(m, m2)
        a = jnp.exp2((m - top) * LOG2E)
        b = jnp.exp2((m2 - top) * LOG2E)
        return num * spread(a) + num2 * spread(b), top, l * a + l2 * b

    num, m, l = lax.fori_loop(1, n, merge, parts(me, num_out, stat_out))
    att[mz] = (num / spread(l)).T.astype(bf)

    def a_copy(i, slot):
        return pltpu.make_async_remote_copy(
            src_ref=att.at[mz], dst_ref=att.at[slot], send_sem=a_send.at[i],
            recv_sem=a_recv.at[slot], device_id={"heads": (mz + i) % nz}, device_id_type=MESH)

    for i in range(1, nz):
        a_copy(i, mz).start()
    for i in range(1, nz):
        z = (mz + i) % nz
        pltpu.make_async_remote_copy(
            src_ref=wo_ref.at[:, pl.ds(0, cols)], dst_ref=wo_in.at[z], send_sem=w_send.at[i],
            recv_sem=w_recv.at[z], device_id={"heads": z}, device_id_type=MESH).wait_recv()
    for i in range(1, n):
        peer = peer_of(me, i, n)
        q_copy(peer, me).wait_send()
        n_copy(peer, me).wait_send()
        t_copy(peer, me).wait_send()
    for i in range(1, nz):
        w_copy(i).wait_send()
    out = jnp.dot(att[mz], wo_ref[:, pl.ds(pl.multiple_of(mz * cols, cols), cols)],
                  preferred_element_type=f32)
    for i in range(1, nz):
        z = (mz + i) % nz
        a_copy(i, z).wait_recv()
        out += jnp.dot(att[z], wo_in[z], preferred_element_type=f32)
    o_ref[...] = out.astype(o_ref.dtype)
    for i in range(1, nz):
        a_copy(i, mz).wait_send()


def shards(n, nz, test_rows, query_weight, keys, values, out_weight):
    count, depth = test_rows.shape
    ctx, width = keys.shape
    cols = out_weight.shape[1] // nz
    bf, f32 = jnp.bfloat16, jnp.float32
    dma = pltpu.SemaphoreType.DMA
    hbm = pl.BlockSpec(memory_space=pltpu.HBM)
    return pl.pallas_call(
        functools.partial(kernel, n, nz, math.gcd(ctx, CHUNK)),
        out_shape=jax.ShapeDtypeStruct((count, cols), bf),
        in_specs=[hbm] * 5,
        out_specs=pl.BlockSpec(memory_space=pltpu.VMEM),
        scratch_shapes=[
            pltpu.VMEM((count, depth), bf),
            pltpu.VMEM((depth, width), bf),
            pltpu.VMEM((ctx, width), bf),
            pltpu.VMEM((ctx, width), bf),
            pltpu.VMEM(out_weight.shape, bf),
            pltpu.VMEM((width, ctx), bf),
            pltpu.VMEM((n, count, width), bf),
            pltpu.VMEM((ctx, 2 * count), f32),
            pltpu.VMEM((ctx, 2 * count), f32),
            pltpu.VMEM((n, width, count), bf),
            pltpu.VMEM((n, 8, count), f32),
            pltpu.VMEM((n, width, count), bf),
            pltpu.VMEM((n, 8, count), f32),
            pltpu.VMEM((nz, count, width), bf),
            pltpu.VMEM((nz, width, cols), bf),
            dma((5,)),
            pltpu.SemaphoreType.REGULAR((max(n.bit_length() - 3, 1),)),
            pltpu.SemaphoreType.REGULAR((max(nz - 2, 1),)),
            dma((n,)), dma((n,)), dma((n,)), dma((n,)), dma((n,)), dma((n,)),
            dma((nz,)), dma((nz,)), dma((nz,)), dma((nz,)),
        ],
        compiler_params=pltpu.CompilerParams(
            collective_id=0, has_side_effects=True, vmem_limit_bytes=55136 * 1024),
    )(test_rows, query_weight, keys, values, out_weight)


def solution(mesh):
    in_specs = (
        P("rows", None),
        P(None, "heads"),
        P("rows", "heads"),
        P("rows", "heads"),
        P("heads", None),
    )
    body = functools.partial(shards, mesh.shape["rows"], mesh.shape["heads"])
    return jax.shard_map(body, mesh=mesh, in_specs=in_specs, out_specs=P("rows", "heads"), check_vma=False)
```

```python
import functools
import math

import jax
import jax.numpy as jnp
from jax import lax
from jax.experimental import pallas as pl
from jax.experimental.pallas import tpu as pltpu
from jax.sharding import PartitionSpec as P

HEAD_DIM = 64
LOG2E = math.log2(math.e)
MESH = pl.DeviceIdType.MESH
CHUNK = 1024


def xor_of(a, b, count):
    total = 0
    bit = 1
    while bit < count:
        one = (a // bit) % 2
        two = (b // bit) % 2
        total = total + bit * (one + two - 2 * one * two)
        bit *= 2
    return total


def near_masks(n):
    return [m for m in range(1, n) if (m >> 1) & ((m >> 1) - 1) == 0]


def turn_order(n):
    near = near_masks(n)
    far = [m for m in range(1, n) if m not in near]
    return near[:3] + far + near[:2:-1]


def peer_of(me, step, n):
    if isinstance(step, int):
        return xor_of(me, turn_order(n)[step - 1], n)
    mask = 0
    for i, m in enumerate(turn_order(n)):
        mask = jnp.where(step == i + 1, m, mask)
    return xor_of(me, mask, n)


def kernel(
    n, nz, chunk,
    x_hbm, wq_hbm, k_hbm, v_hbm, wo_hbm, o_ref,
    x_ref, wq_ref, k_ref, v_ref, wo_ref, vt_ref, qall, s0, s1,
    num_out, stat_out, num_in, stat_in, att, wo_in,
    in_sem, row_sem, col_sem, q_send, q_recv, n_send, n_recv, t_send, t_recv, a_send, a_recv, w_send, w_recv,
):
    me = lax.axis_index("rows")
    mz = lax.axis_index("heads")
    count = x_ref.shape[0]
    ctx, width = k_ref.shape
    cols = o_ref.shape[1]
    f32, bf = jnp.float32, jnp.bfloat16
    chunks = [pl.ds(c, chunk) for c in range(0, ctx, chunk)]

    loads = [
        pltpu.make_async_copy(src, dst, in_sem.at[i])
        for i, (src, dst) in enumerate([
            (x_hbm, x_ref), (wq_hbm, wq_ref), (k_hbm, k_ref), (v_hbm, v_ref), (wo_hbm, wo_ref)])]
    for load in loads:
        load.start()

    near = near_masks(n)
    below = (mz + nz - 1) // nz
    above = (2 * nz - 2 - mz) // nz

    def tell_columns(sem):
        @pl.when(mz > 0)
        def _():
            pl.semaphore_signal(sem, inc=1, device_id={"heads": mz - 1}, device_id_type=MESH)

        @pl.when(mz < nz - 1)
        def _():
            pl.semaphore_signal(sem, inc=1, device_id={"heads": mz + 1}, device_id_type=MESH)

    def tell_rows(sem):
        for m in spread_by:
            pl.semaphore_signal(sem, inc=1, device_id={"rows": xor_of(me, m, n)}, device_id_type=MESH)

    spread_by = [m for m in near if m > 1 and m % 2 == 0]
    barrier = pltpu.get_barrier_semaphore()
    for m in near:
        pl.semaphore_signal(barrier, inc=1, device_id={"rows": xor_of(me, m, n)}, device_id_type=MESH)
    tell_columns(barrier)

    loads[0].wait()
    loads[1].wait()
    q = jnp.dot(x_ref[...], wq_ref[...], preferred_element_type=f32).astype(bf)
    qall[me] = q * jnp.bfloat16(HEAD_DIM ** -0.5)

    def q_copy(peer, slot):
        return pltpu.make_async_remote_copy(
            src_ref=qall.at[me], dst_ref=qall.at[slot], send_sem=q_send.at[peer],
            recv_sem=q_recv.at[slot], device_id={"rows": peer}, device_id_type=MESH)

    def w_copy(i):
        peer = (mz + i) % nz
        return pltpu.make_async_remote_copy(
            src_ref=wo_ref.at[:, pl.ds(pl.multiple_of(peer * cols, cols), cols)],
            dst_ref=wo_in.at[mz], send_sem=w_send.at[i], recv_sem=w_recv.at[mz],
            device_id={"heads": peer}, device_id_type=MESH)

    lane = lax.broadcasted_iota(jnp.int32, (1, width), 1)
    keep0 = jnp.where(lane < HEAD_DIM, 1.0, 0.0).astype(bf)
    keep1 = jnp.where(lane < HEAD_DIM, 0.0, 1.0).astype(bf)

    def both_heads(peer):
        q = qall[peer]
        return jnp.concatenate([q * keep0, q * keep1], axis=0)

    def score(both, part, s_ref, top):
        s = lax.dot_general(k_ref[part, :], both, (((1,), (1,)), ((), ())), preferred_element_type=f32)
        s_ref[part, :] = s
        here = jnp.max(s, axis=0, keepdims=True)
        return here if top is None else jnp.maximum(top, here)

    def weigh(s_ref, part, top, acc):
        w = jnp.exp2((s_ref[part, :] - top) * LOG2E)
        summed = jnp.dot(vt_ref[:, part], w.astype(bf), preferred_element_type=f32)
        return summed if acc is None else acc + summed

    def keep(peer, top, total, acc):
        num = jnp.concatenate([acc[:HEAD_DIM, :count], acc[HEAD_DIM:, count:]], axis=0)
        num_out[peer] = num.astype(num_out.dtype)
        stat_out[peer, 0:1, :] = top[:, :count]
        stat_out[peer, 1:2, :] = top[:, count:]
        stat_out[peer, 2:3, :] = total[:, :count]
        stat_out[peer, 3:4, :] = total[:, count:]

    def turn(now, s_now, top, later, s_later):
        both = None if later is None else both_heads(later)
        after = acc = None
        for part in chunks:
            if both is not None:
                after = score(both, part, s_later, after)
            acc = weigh(s_now, part, top, acc)
        keep(now, top, acc[width:width + 1], acc[:width])
        return after

    def n_copy(peer, slot):
        return pltpu.make_async_remote_copy(
            src_ref=num_out.at[peer], dst_ref=num_in.at[slot], send_sem=n_send.at[peer],
            recv_sem=n_recv.at[slot], device_id={"rows": peer}, device_id_type=MESH)

    def t_copy(peer, slot):
        return pltpu.make_async_remote_copy(
            src_ref=stat_out.at[peer], dst_ref=stat_in.at[slot], send_sem=t_send.at[peer],
            recv_sem=t_recv.at[slot], device_id={"rows": peer}, device_id_type=MESH)

    def send(peer):
        n_copy(peer, me).start()
        t_copy(peer, me).start()

    def await_q(step):
        peer = peer_of(me, step, n)
        q_copy(peer, peer).wait_recv()
        return peer

    stat_out[...] = jnp.zeros(stat_out.shape, f32)
    pl.semaphore_wait(barrier, len(near) + below + above)
    if len(spread_by) > 1:
        tell_rows(row_sem.at[0])
    if nz > 2:
        tell_columns(col_sem.at[0])
    for m in turn_order(n):
        if m in near:
            q_copy(xor_of(me, m, n), me).start()

    loads[2].wait()
    loads[3].wait()
    both = both_heads(me)
    top = None
    for part in chunks:
        top = score(both, part, s0, top)
        vt_ref[:width, part] = v_ref[part, :].T
        vt_ref[width:, part] = jnp.ones((16, chunk), bf)

    for i in range(len(spread_by) - 1):
        pl.semaphore_wait(row_sem.at[i], len(spread_by))
        if i + 1 < len(spread_by) - 1:
            tell_rows(row_sem.at[i + 1])
    for m in turn_order(n):
        if m not in near:
            q_copy(xor_of(me, m, n), me).start()
    for i in range(nz - 3):
        pl.semaphore_wait(col_sem.at[i], below + above)
        tell_columns(col_sem.at[i + 1])

    turn(me, s0, top, None, None)

    both = both_heads(await_q(1))
    top = None
    for part in chunks:
        top = score(both, part, s1, top)

    def share_weights():
        if nz > 2:
            pl.semaphore_wait(col_sem.at[nz - 3], below + above)
        loads[4].wait()
        for i in range(1, nz):
            w_copy(i).start()

    def two(pair, top):
        step = 2 * pair + 1
        now, later = peer_of(me, step, n), await_q(step + 1)
        top = turn(now, s1, top, later, s0)
        send(now)

        @pl.when(pair == 0)
        def _():
            share_weights()

        now, later = later, await_q(step + 2)
        top = turn(now, s0, top, later, s1)
        send(now)
        return top

    if n == 2:
        share_weights()
    top = lax.fori_loop(0, (n - 2) // 2, two, top)
    last = peer_of(me, n - 1, n)
    turn(last, s1, top, None, None)
    send(last)

    def parts(peer, num_ref, stat_ref):
        return (num_ref[peer].astype(f32), stat_ref[peer, 0:2, :], stat_ref[peer, 2:4, :])

    def spread(pair):
        return jnp.concatenate([
            jnp.broadcast_to(pair[0:1, :], (HEAD_DIM, count)),
            jnp.broadcast_to(pair[1:2, :], (HEAD_DIM, count))], axis=0)

    def merge(step, state):
        num, m, l = state
        peer = peer_of(me, step, n)
        n_copy(peer, peer).wait_recv()
        t_copy(peer, peer).wait_recv()
        num2, m2, l2 = parts(peer, num_in, stat_in)
        top = jnp.maximum(m, m2)
        a = jnp.exp2((m - top) * LOG2E)
        b = jnp.exp2((m2 - top) * LOG2E)
        return num * spread(a) + num2 * spread(b), top, l * a + l2 * b

    num, m, l = lax.fori_loop(1, n, merge, parts(me, num_out, stat_out))
    att[mz] = (num / spread(l)).T.astype(bf)

    def a_copy(i, slot):
        return pltpu.make_async_remote_copy(
            src_ref=att.at[mz], dst_ref=att.at[slot], send_sem=a_send.at[i],
            recv_sem=a_recv.at[slot], device_id={"heads": (mz + i) % nz}, device_id_type=MESH)

    for i in range(1, nz):
        a_copy(i, mz).start()
    for i in range(1, nz):
        z = (mz + i) % nz
        pltpu.make_async_remote_copy(
            src_ref=wo_ref.at[:, pl.ds(0, cols)], dst_ref=wo_in.at[z], send_sem=w_send.at[i],
            recv_sem=w_recv.at[z], device_id={"heads": z}, device_id_type=MESH).wait_recv()
    for i in range(1, n):
        peer = peer_of(me, i, n)
        q_copy(peer, me).wait_send()
        n_copy(peer, me).wait_send()
        t_copy(peer, me).wait_send()
    for i in range(1, nz):
        w_copy(i).wait_send()
    out = jnp.dot(att[mz], wo_ref[:, pl.ds(pl.multiple_of(mz * cols, cols), cols)],
                  preferred_element_type=f32)
    for i in range(1, nz):
        z = (mz + i) % nz
        a_copy(i, z).wait_recv()
        out += jnp.dot(att[z], wo_in[z], preferred_element_type=f32)
    o_ref[...] = out.astype(o_ref.dtype)
    for i in range(1, nz):
        a_copy(i, mz).wait_send()


def shards(n, nz, test_rows, query_weight, keys, values, out_weight):
    count, depth = test_rows.shape
    ctx, width = keys.shape
    cols = out_weight.shape[1] // nz
    bf, f32 = jnp.bfloat16, jnp.float32
    dma = pltpu.SemaphoreType.DMA
    hbm = pl.BlockSpec(memory_space=pltpu.HBM)
    return pl.pallas_call(
        functools.partial(kernel, n, nz, math.gcd(ctx, CHUNK)),
        out_shape=jax.ShapeDtypeStruct((count, cols), bf),
        in_specs=[hbm] * 5,
        out_specs=pl.BlockSpec(memory_space=pltpu.VMEM),
        scratch_shapes=[
            pltpu.VMEM((count, depth), bf),
            pltpu.VMEM((depth, width), bf),
            pltpu.VMEM((ctx, width), bf),
            pltpu.VMEM((ctx, width), bf),
            pltpu.VMEM(out_weight.shape, bf),
            pltpu.VMEM((width + 16, ctx), bf),
            pltpu.VMEM((n, count, width), bf),
            pltpu.VMEM((ctx, 2 * count), f32),
            pltpu.VMEM((ctx, 2 * count), f32),
            pltpu.VMEM((n, width, count), bf),
            pltpu.VMEM((n, 8, count), f32),
            pltpu.VMEM((n, width, count), bf),
            pltpu.VMEM((n, 8, count), f32),
            pltpu.VMEM((nz, count, width), bf),
            pltpu.VMEM((nz, width, cols), bf),
            dma((5,)),
            pltpu.SemaphoreType.REGULAR((max(n.bit_length() - 3, 1),)),
            pltpu.SemaphoreType.REGULAR((max(nz - 2, 1),)),
            dma((n,)), dma((n,)), dma((n,)), dma((n,)), dma((n,)), dma((n,)),
            dma((nz,)), dma((nz,)), dma((nz,)), dma((nz,)),
        ],
        compiler_params=pltpu.CompilerParams(
            collective_id=0, has_side_effects=True, vmem_limit_bytes=55136 * 1024),
    )(test_rows, query_weight, keys, values, out_weight)


def solution(mesh):
    in_specs = (
        P("rows", None),
        P(None, "heads"),
        P("rows", "heads"),
        P("rows", "heads"),
        P("heads", None),
    )
    body = functools.partial(shards, mesh.shape["rows"], mesh.shape["heads"])
    return jax.shard_map(body, mesh=mesh, in_specs=in_specs, out_specs=P("rows", "heads"), check_vma=False)
```
